256 devices in a mesh: seq: 32 (over y, x, core), head: 8 (over z).
Axes of the slice: x: 4, y: 4, z: 8, core: 2. Of those that a mesh axis runs over, the one named last changes fastest.
Arguments:
- queries: bfloat16 [32768, 8192], P(('seq', 'head')), may hold values from -6 to 6
- key_vectors: bfloat16 [32768, 8192], P(('seq', 'head')), may hold values from -6 to 6
- value_vectors: bfloat16 [32768, 8192], P(('seq', 'head')), may hold values from -6 to 6
- out_gain: float32 [64, 128], P('head'), may hold values from 0.1 to 1.9
Outputs:
- attended: bfloat16 [32768, 8192], P(('seq', 'head'))
The draws below stay inside these ranges and needn't reach their ends.
All inputs are finite; a program needn't handle non-finite values.
Results may differ from the reference program's by a relative error of at most 0.0049.
Values may be sent and summed in bfloat16 or wider, within the bound.
A program may use at most 128 MiB of HBM per device.

```python
import jax
import jax.numpy as jnp
from jax import lax

HEADS = 64
HD = 128
BLOCK = 512
SEQLEN = 32768


def steps_of(own_key, dims, split, low, top_value):
    factor_of, own = 1.0, jax.random.fold_in(own_key, 6)
    for dim, blocks in split:
        draws = jnp.exp(jax.random.uniform(jax.random.fold_in(own, dim), (blocks,), jnp.float32, low / len(split), top_value / len(split)))
        factor_of = factor_of * jnp.repeat(draws, dims[dim] // blocks).reshape([-1 if axis == dim else 1 for axis in range(len(dims))])
    return factor_of


def gaussian(rng, extent, spread, bound, split=(), kind=jnp.bfloat16):
    drawn = spread * jax.random.normal(rng, extent, jnp.float32)
    if split:
        drawn = drawn * steps_of(rng, extent, split, -0.22, 0.18)
    return jnp.clip(drawn, -bound, bound).astype(kind)


def setup_inputs(seed: int = 0) -> dict:
    arg_keys = jax.random.split(jax.random.key(seed), 5)
    return {
        "queries": gaussian(arg_keys[0], (SEQLEN, HEADS * HD), 1.0, 6.0, ((0, 256),)),
        "key_vectors": gaussian(arg_keys[1], (SEQLEN, HEADS * HD), 1.0, 6.0, ((0, 256),)),
        "value_vectors": gaussian(arg_keys[2], (SEQLEN, HEADS * HD), 1.0, 6.0, ((0, 256),)),
        "out_gain": jnp.clip(1.0 + 0.18 * jax.random.normal(arg_keys[3], (HEADS, HD), jnp.float32), 0.1, 1.9),
    }


def reference(queries, key_vectors, value_vectors, out_gain):
    count = queries.shape[0] // BLOCK
    query_blocks = queries.reshape(count, BLOCK, HEADS, HD)
    key_blocks = key_vectors.reshape(count, BLOCK, HEADS, HD)
    value_blocks = value_vectors.reshape(count, BLOCK, HEADS, HD)
    causal = jnp.arange(BLOCK)[:, None] >= jnp.arange(BLOCK)[None, :]
    highest = lax.Precision.HIGHEST

    def one_head(index):
        query_f = lax.dynamic_index_in_dim(query_blocks, index, 2, keepdims=False).astype(jnp.float32)
        key_f = lax.dynamic_index_in_dim(key_blocks, index, 2, keepdims=False).astype(jnp.float32)
        value_f = lax.dynamic_index_in_dim(value_blocks, index, 2, keepdims=False).astype(jnp.float32)
        states = jnp.einsum('nbd,nbe->nde', key_f, value_f, precision=highest)
        carried = (jnp.cumsum(states, axis=0) - states).astype(jnp.bfloat16)
        carried = lax.optimization_barrier(carried).astype(jnp.float32)
        inter = jnp.einsum('nbd,nde->nbe', query_f, carried, precision=highest)
        scores = jnp.einsum('nbd,ncd->nbc', query_f, key_f, precision=highest)
        scores = jnp.where(causal[None], scores, jnp.float32(0.0)).astype(jnp.bfloat16)
        scores = lax.optimization_barrier(scores).astype(jnp.float32)
        intra = jnp.einsum('nbc,ncd->nbd', scores, value_f, precision=highest)
        raw = inter + intra
        gain_row = lax.dynamic_index_in_dim(out_gain, index, 0, keepdims=False)
        scale = lax.rsqrt(lax.optimization_barrier(jnp.mean(raw * raw, axis=-1, keepdims=True)) + 1e-06)
        return (raw * scale * gain_row).astype(jnp.bfloat16)
    result = lax.map(one_head, jnp.arange(HEADS, dtype=jnp.int32))
    result = jnp.transpose(result, (1, 2, 0, 3))
    return result.reshape(count * BLOCK, HEADS * HD)
```

```python
import jax
import jax.numpy as jnp
from jax import lax
from jax.sharding import PartitionSpec as P

HEADS = 64
HD = 128


def shifted(block, axis, distance):
    count = lax.axis_size(axis)
    return lax.ppermute(block, axis, [(i, i + distance) for i in range(count - distance)])


def seq_exclusive(own):
    count = lax.axis_size("seq")
    total = own
    distance = 1
    while distance < count:
        total = total + shifted(total, "seq", distance)
        distance *= 2
    return shifted(total, "seq", 1)


def per_device(queries, key_vectors, value_vectors, out_gain):
    tokens = queries.shape[0]
    query_heads = queries.reshape(tokens, HEADS, HD)
    key_heads = key_vectors.reshape(tokens, HEADS, HD)
    value_heads = value_vectors.reshape(tokens, HEADS, HD)
    states = jnp.einsum("bhd,bhe->hde", key_heads, value_heads, preferred_element_type=jnp.float32)
    gathered = lax.all_to_all(
        states.astype(jnp.bfloat16).reshape(8, HEADS // 8, HD, HD), "head", split_axis=0, concat_axis=0, tiled=True
    ).astype(jnp.float32)
    gain = lax.all_gather(out_gain, "head", axis=0, tiled=True)
    prefix = seq_exclusive(jnp.sum(gathered, axis=0))
    running = prefix
    parts = []
    for z in range(8):
        parts.append(running.astype(jnp.bfloat16))
        running = running + gathered[z]
    carried = lax.all_to_all(jnp.stack(parts), "head", split_axis=0, concat_axis=0, tiled=True)
    carried = carried.reshape(HEADS, HD, HD)
    inter = jnp.einsum("bhd,hde->bhe", query_heads, carried, preferred_element_type=jnp.float32)
    scores = jnp.einsum("bhd,chd->hbc", query_heads, key_heads, preferred_element_type=jnp.float32)
    causal = jnp.arange(tokens)[:, None] >= jnp.arange(tokens)[None, :]
    scores = jnp.where(causal[None], scores, jnp.float32(0.0)).astype(jnp.bfloat16)
    intra = jnp.einsum("hbc,chd->bhd", scores, value_heads, preferred_element_type=jnp.float32)
    raw = inter + intra
    scale = lax.rsqrt(jnp.mean(raw * raw, axis=-1, keepdims=True) + 1e-06)
    normed = (raw * scale * gain[None]).astype(jnp.bfloat16)
    return normed.reshape(tokens, HEADS * HD)


def solution(mesh):
    return jax.shard_map(
        per_device,
        mesh=mesh,
        in_specs=(
            P(("seq", "head"), None),
            P(("seq", "head"), None),
            P(("seq", "head"), None),
            P("head", None),
        ),
        out_specs=P(("seq", "head"), None),
        check_vma=False,
    )
```

```python
import functools

import jax
import jax.numpy as jnp
from jax import lax
from jax.experimental import pallas as pl
from jax.experimental.pallas import tpu as pltpu
from jax.sharding import PartitionSpec as P

HEADS = 64
HD = 128
TOK = 128
Z = 8
LINE = 16
CHUNKS = HEADS // LINE
MESH = pl.DeviceIdType.MESH
BF16 = jnp.bfloat16
F32 = jnp.float32


def columns(head):
    return pl.ds(pl.multiple_of(head * HD, HD), HD)


def kernel(
    q_ref,
    k_ref,
    v_ref,
    gain_ref,
    out_ref,
    state_send,
    state_recv,
    row_send,
    row_recv,
    col_send,
    col_recv,
    carry_send,
    carry_recv,
    gain_all,
    intra,
    state_ssem,
    state_rsem,
    row_ssem,
    row_rsem,
    col_ssem,
    col_rsem,
    carry_ssem,
    carry_rsem,
    gain_ssem,
    gain_rsem,
):
    seq = lax.axis_index("seq")
    z = lax.axis_index("head")
    core = lax.rem(seq, 2)
    chip = seq - core
    x = lax.rem(seq // 2, 4)
    y = seq // 8
    me = core * Z + z

    def line_peer(dz, dc):
        other_core = lax.rem(core + dc, 2)
        other_z = lax.rem(z + dz, Z)
        return (chip + other_core, other_z), other_core * Z + other_z

    def row_peer(d):
        other = lax.rem(x + d, 4)
        return (y * 8 + other * 2 + core, z), other

    def col_peer(d):
        other = lax.rem(y + d, 4)
        return (other * 8 + x * 2 + core, z), other

    offsets = [(dz, dc) for dz in (4, 3, 5, 2, 6, 1, 7, 0) for dc in (0, 1) if (dz, dc) != (0, 0)]

    barrier = pltpu.get_barrier_semaphore()
    for dz, dc in offsets:
        pl.semaphore_signal(barrier, inc=1, device_id=line_peer(dz, dc)[0], device_id_type=MESH)
    for d in (1, 2, 3):
        pl.semaphore_signal(barrier, inc=1, device_id=row_peer(d)[0], device_id_type=MESH)
        pl.semaphore_signal(barrier, inc=1, device_id=col_peer(d)[0], device_id_type=MESH)
    pl.semaphore_wait(barrier, len(offsets) + 6)

    def gain_copy(dz):
        target, _ = line_peer(dz, 0)
        return pltpu.make_async_remote_copy(
            src_ref=gain_ref,
            dst_ref=gain_all.at[z],
            send_sem=gain_ssem.at[target[1]],
            recv_sem=gain_rsem.at[z],
            device_id=target,
            device_id_type=MESH,
        )

    def gain_arrival(dz):
        source = lax.rem(z + dz, Z)
        return pltpu.make_async_remote_copy(
            src_ref=gain_ref,
            dst_ref=gain_all.at[source],
            send_sem=gain_ssem.at[source],
            recv_sem=gain_rsem.at[source],
            device_id=line_peer(dz, 0)[0],
            device_id_type=MESH,
        )

    def line_copy(send, recv, ssem, rsem, j, dz, dc, slot):
        target, index = line_peer(dz, dc)
        return pltpu.make_async_remote_copy(
            src_ref=send.at[j, index],
            dst_ref=recv.at[j, slot(index)],
            send_sem=ssem.at[j, index],
            recv_sem=rsem.at[j, slot(index)],
            device_id=target,
            device_id_type=MESH,
        )

    mine = lambda index: me
    theirs = lambda index: index

    def side_copy(send, recv, ssem, rsem, j, peer, slot, d):
        return pltpu.make_async_remote_copy(
            src_ref=send.at[j],
            dst_ref=recv.at[j, slot],
            send_sem=ssem.at[j, d],
            recv_sem=rsem.at[j, slot],
            device_id=peer,
            device_id_type=MESH,
        )

    def make_states(j):
        def state(index):
            cols = columns(index * CHUNKS + j)
            return lax.dot_general(
                k_ref[:, cols], v_ref[:, cols], (((0,), (0,)), ((), ())), preferred_element_type=F32
            ).astype(BF16)

        for dz, dc in offsets:
            _, index = line_peer(dz, dc)
            state_send[j, index] = state(index)
            line_copy(state_send, state_recv, state_ssem, state_rsem, j, dz, dc, mine).start()
        state_recv[j, me] = state(me)

    def reduce_line(j):
        for dz, dc in offsets:
            line_copy(state_send, state_recv, state_ssem, state_rsem, j, dz, dc, theirs).wait_recv()
        total = state_recv[j, 0].astype(F32)
        for index in range(1, LINE):
            total = total + state_recv[j, index].astype(F32)
        row_send[j] = total
        for d in (1, 2, 3):
            side_copy(row_send, row_recv, row_ssem, row_rsem, j, row_peer(d)[0], x, d).start()

    def reduce_row(j):
        for d in (1, 2, 3):
            peer, other = row_peer(d)
            side_copy(row_send, row_recv, row_ssem, row_rsem, j, peer, other, d).wait_recv()
        total = row_send[j]
        before = jnp.zeros((HD, HD), F32)
        for d in (1, 2, 3):
            _, other = row_peer(d)
            value = row_recv[j, other]
            total = total + value
            before = before + jnp.where(other < x, value, 0.0)
        col_send[j] = total
        row_recv[j, x] = before
        for d in (1, 2, 3):
            side_copy(col_send, col_recv, col_ssem, col_rsem, j, col_peer(d)[0], y, d).start()

    def spread(j):
        for d in (1, 2, 3):
            peer, other = col_peer(d)
            side_copy(col_send, col_recv, col_ssem, col_rsem, j, peer, other, d).wait_recv()
        running = row_recv[j, x]
        for d in (1, 2, 3):
            _, other = col_peer(d)
            running = running + jnp.where(other < y, col_recv[j, other], 0.0)
        for index in range(LINE):
            carry_send[j, index] = running.astype(BF16)
            running = running + state_recv[j, index].astype(F32)
        for dz, dc in offsets:
            line_copy(carry_send, carry_recv, carry_ssem, carry_rsem, j, dz, dc, mine).start()
        carry_recv[j, me] = carry_send[j, me]

    causal = lax.broadcasted_iota(jnp.int32, (TOK, TOK), 0) >= lax.broadcasted_iota(jnp.int32, (TOK, TOK), 1)

    def local_heads(j):
        for index in range(LINE):
            cols = columns(index * CHUNKS + j)
            scores = lax.dot_general(
                q_ref[:, cols], k_ref[:, cols], (((1,), (1,)), ((), ())), preferred_element_type=F32
            )
            scores = jnp.where(causal, scores, 0.0).astype(BF16)
            intra[:, cols] = jnp.dot(scores, v_ref[:, cols], preferred_element_type=F32)

    def finish(j):
        for dz, dc in offsets:
            line_copy(carry_send, carry_recv, carry_ssem, carry_rsem, j, dz, dc, theirs).wait_recv()
        for index in range(LINE):
            owner = index
            head = (index * CHUNKS) + j
            cols = columns(head)
            raw = intra[:, cols] + jnp.dot(q_ref[:, cols], carry_recv[j, owner], preferred_element_type=F32)
            scale = lax.rsqrt(jnp.mean(raw * raw, axis=-1, keepdims=True) + 1e-06)
            gain = gain_all[index * CHUNKS // 8, pl.ds(lax.rem(index * CHUNKS, 8) + j, 1), :]
            out_ref[:, cols] = (raw * scale * gain).astype(BF16)

    for dz in range(1, Z):
        gain_copy(dz).start()
    gain_all[z] = gain_ref[...]

    lax.fori_loop(0, CHUNKS, lambda j, _: (make_states(j), None)[1], None)
    lax.fori_loop(0, CHUNKS, lambda j, _: (local_heads(j), None)[1], None)

    def wave(t, _):
        @pl.when(t < CHUNKS)
        def _():
            reduce_line(t)

        @pl.when(jnp.logical_and(t >= 2, t < CHUNKS + 2))
        def _():
            spread(t - 2)

        @pl.when(jnp.logical_and(t >= 1, t < CHUNKS + 1))
        def _():
            reduce_row(t - 1)

    lax.fori_loop(0, CHUNKS + 2, wave, None)
    for dz in range(1, Z):
        gain_arrival(dz).wait_recv()
    lax.fori_loop(0, CHUNKS, lambda j, _: (finish(j), None)[1], None)

    def drain(j, _):
        for dz, dc in offsets:
            line_copy(state_send, state_recv, state_ssem, state_rsem, j, dz, dc, mine).wait_send()
            line_copy(carry_send, carry_recv, carry_ssem, carry_rsem, j, dz, dc, mine).wait_send()
        for d in (1, 2, 3):
            side_copy(row_send, row_recv, row_ssem, row_rsem, j, row_peer(d)[0], x, d).wait_send()
            side_copy(col_send, col_recv, col_ssem, col_rsem, j, col_peer(d)[0], y, d).wait_send()

    lax.fori_loop(0, CHUNKS, drain, None)
    for dz in range(1, Z):
        gain_copy(dz).wait_send()


def per_device(queries, key_vectors, value_vectors, out_gain):
    vmem = pl.BlockSpec(memory_space=pltpu.VMEM)
    dma = pltpu.SemaphoreType.DMA
    return pl.pallas_call(
        kernel,
        out_shape=jax.ShapeDtypeStruct((TOK, HEADS * HD), BF16),
        in_specs=[vmem] * 4,
        out_specs=vmem,
        scratch_shapes=[
            pltpu.VMEM((CHUNKS, LINE, HD, HD), BF16),
            pltpu.VMEM((CHUNKS, LINE, HD, HD), BF16),
            pltpu.VMEM((CHUNKS, HD, HD), F32),
            pltpu.VMEM((CHUNKS, 4, HD, HD), F32),
            pltpu.VMEM((CHUNKS, HD, HD), F32),
            pltpu.VMEM((CHUNKS, 4, HD, HD), F32),
            pltpu.VMEM((CHUNKS, LINE, HD, HD), BF16),
            pltpu.VMEM((CHUNKS, LINE, HD, HD), BF16),
            pltpu.VMEM((Z, 8, HD), F32),
            pltpu.VMEM((TOK, HEADS * HD), F32),
            dma((CHUNKS, LINE)),
            dma((CHUNKS, LINE)),
            dma((CHUNKS, 4)),
            dma((CHUNKS, 4)),
            dma((CHUNKS, 4)),
            dma((CHUNKS, 4)),
            dma((CHUNKS, LINE)),
            dma((CHUNKS, LINE)),
            dma((Z,)),
            dma((Z,)),
        ],
        compiler_params=pltpu.CompilerParams(
            collective_id=0, has_side_effects=True, vmem_limit_bytes=48 * 1024 * 1024
        ),
    )(queries, key_vectors, value_vectors, out_gain)


def solution(mesh):
    return jax.shard_map(
        per_device,
        mesh=mesh,
        in_specs=(
            P(("seq", "head"), None),
            P(("seq", "head"), None),
            P(("seq", "head"), None),
            P("head", None),
        ),
        out_specs=P(("seq", "head"), None),
        check_vma=False,
    )
```
